32 devices in a mesh: groups: 2 (over y), ep: 16 (over z, x, core).
Axes of the slice: x: 2, y: 2, z: 4, core: 2. Of those that a mesh axis runs over, the one named last changes fastest.
Arguments:
- queries: bfloat16 [64, 128, 576], P(('groups', 'ep')), parts along dimension 0, may hold values from -120 to 120
- kv_cache: bfloat16 [64, 256, 576], P(('groups', 'ep')), parts along dimension 0, may hold values from -6 to 6
- kv_lengths: int32 [64], P(('groups', 'ep')), parts along dimension 0, may hold values from 32 to 256, as said below
- moe_input: bfloat16 [64, 7168], P(('groups', 'ep')), parts along dimension 0, may hold values from -6 to 6
- expert_ids: int32 [64, 8], P(('groups', 'ep')), parts along dimension 0, may hold values from 0 to 15, all different within a row; in each aligned block of 2 rows (0 to 1, 2 to 3, ...) at most 2 rows name the same one
- route_weights: float32 [64, 8], P(('groups', 'ep')), parts along dimension 0, may hold values from 0.1 to 1
- w_gate: bfloat16 [32768, 7168], P('ep'), may hold values from -0.0625 to 0.0625
- w_up: bfloat16 [32768, 7168], P('ep'), may hold values from -0.0625 to 0.0625
- w_down: bfloat16 [32768, 7168], P('ep'), may hold values from -0.125 to 0.125
Outputs:
- attended: bfloat16 [64, 128, 512], P(('groups', 'ep')), parts along dimension 0
- moe_output: bfloat16 [64, 7168], P(('groups', 'ep')), parts along dimension 0
The draws below stay inside these ranges and needn't reach their ends.
There are 2 independent parts, one for each index of `groups`. The reference program is written for one: setup_inputs(seed, part) draws one part's arguments, and reference() takes and returns one part's arrays. A program takes and returns all parts, laid end to end along the dimension named above; an argument that names none is the same for every part. Nothing has to cross between parts.
Inputs may be any that keep to these rules, and one draw needn't show every extreme that they name: `expert_ids`: the 8 ids of a row differ. Among the 2 rows of one device no expert is named more than 2 times, and in every draw some expert is named exactly 2 times by the rows of some device. `kv_lengths`: some request in every draw uses all 256 slots.
All inputs are finite; a program needn't handle non-finite values.
Results may differ from the reference program's by a relative error of at most 0.0085.
Values may be sent and summed in bfloat16 or wider, within the bound.
No kernel may reach another device: no remote copies, remote signals or barrier semaphores. Data moves between devices by JAX's collectives and lax.ppermute only.
A program may use at most 128 MiB of HBM per device.

```python
import math
import jax
import jax.numpy as jnp
import numpy as np
from jax import lax

D = 7168
FF = 2048
HEADS = 128
LAT = 512
ROPE = 64
TOPK = 8
EXPERTS = 16
REQ_DEV = 2
LMAX = 256
CAP = 2
TOKENS = 32
N_EP = 16


def cache_field(key):
    base = jax.random.fold_in(key, 11)
    field = jnp.clip(jax.random.normal(base, (TOKENS, LMAX, LAT + ROPE), jnp.float32), -6.0, 6.0)
    return field


def draw_kv_cache(key, part):
    return cache_field(key).astype(jnp.bfloat16)


def draw_queries(key, part):
    base = jax.random.fold_in(key, 23)
    field = jnp.clip(jax.random.normal(base, (TOKENS, HEADS, LAT + ROPE), jnp.float32), -6.0, 6.0)
    return field.astype(jnp.bfloat16)


def draw_kv_lengths(key, part):
    base = jax.random.fold_in(key, 37)
    lengths = jax.random.randint(base, (TOKENS,), max(2, LMAX // 8), LMAX + 1).astype(jnp.int32)
    return lengths.at[0].set(LMAX)


def levels(stream_key, dims, split, least, top_value):
    def one(dim, blocks):
        draws = jax.random.uniform(jax.random.fold_in(jax.random.fold_in(stream_key, 6), dim), (blocks,), jnp.float32, least / len(split), top_value / len(split))
        return jnp.repeat(jnp.exp(draws), dims[dim] // blocks).reshape((-1,) + (1,) * (len(dims) - dim - 1))

    gain = one(*split[0])
    for cut in split[1:]:
        gain = gain * one(*cut)
    return gain


def deal_out(key, own, number, rows, count, top, bound, skew):
    sequence = jax.random.permutation(key, count)
    crowded, common = shares(count, rows * top, bound, skew, True), shares(count, rows * top, bound, skew, False)
    places = jnp.arange(count)

    def named(tallies, rotation):
        used = int((tallies > 0).sum())
        fixed = max(1, used // 4)
        moved = fixed + (places - fixed + rotation * (used - fixed)) % max(1, count - fixed)
        return jnp.zeros((count,), jnp.int32).at[sequence[jnp.where(places < fixed, places, moved)]].set(jnp.asarray(tallies, jnp.int32))

    tallies = jnp.where(number % 4 == 0, named(crowded, number // 4), named(common, number - number // 4 - 1))
    mixed = jax.random.permutation(jax.random.fold_in(own, 3), count)
    donor, receiver = mixed[0:count // 2 * 2:2], mixed[1:count // 2 * 2:2]
    slack = jnp.minimum(tallies[donor] - 1, bound - tallies[receiver]) // 2
    slack = jnp.where((donor == sequence[0]) | (receiver == sequence[0]) | (tallies[receiver] == 0), 0, jnp.maximum(slack, 0))
    moved = jax.random.randint(jax.random.fold_in(own, 4), (count // 2,), 0, 1 << 20) % (slack + 1)
    tallies = tallies.at[donor].add(-moved).at[receiver].add(moved)
    items = jnp.searchsorted(jnp.cumsum(tallies), jnp.arange(rows * top), side="right").astype(jnp.int32)
    grid = items.reshape(top, rows).T
    grid = grid[jax.random.permutation(jax.random.fold_in(own, 1), rows)]
    rotation = jax.random.randint(jax.random.fold_in(own, 2), (rows, 1), 0, top)
    return jnp.take_along_axis(grid, (jnp.arange(top)[None, :] + rotation) % top, axis=1)


def shares(count, total, most, slope, full):
    weights = [(1 << 20) // math.isqrt(rank ** slope) + 1 for rank in range(1, count + 1)]
    largest = most if full else min(most, max(-(-total // count), total * weights[0] // sum(weights)))
    least = 1 if total - largest >= count - 1 else 0
    holding, rest = [largest] + [least] * (count - 1), total - largest - least * (count - 1)
    while rest > 0:
        movable = [i for i in range(1, count) if holding[i] < largest] or [i for i in range(1, count) if holding[i] < most]
        pool, budget = sum([weights[i] for i in movable]), rest
        for i in movable:
            extra = min(most - holding[i], max(1, budget * weights[i] // pool), rest)
            holding[i] = holding[i] + extra
            rest = rest - extra
    return np.array(holding)


def gaussian(rng, dims, scale, reach, pieces=(), kind=jnp.bfloat16):
    level = levels(rng, dims, pieces, -0.22, 0.18) if pieces else 1.0
    drawn = jax.random.normal(rng, dims, jnp.float32) * scale * level
    return jnp.minimum(jnp.maximum(drawn, -reach), reach).astype(kind)


def setup_inputs(seed: int = 0, part: int = 0) -> dict:
    streams_of = jax.random.split(jax.random.key(seed), 10)
    part_keys = jax.random.split(jax.random.fold_in(streams_of[9], part), 10)
    queries = draw_queries(jax.random.fold_in(jax.random.fold_in(streams_of[9], part), 71), part)
    kv_cache = draw_kv_cache(jax.random.fold_in(jax.random.fold_in(streams_of[9], part), 71), part)
    kv_lengths = draw_kv_lengths(jax.random.fold_in(jax.random.fold_in(streams_of[9], part), 71), part)
    moe_input = gaussian(part_keys[3], (TOKENS, D), 1.0, 6.0, ((0, 16),))
    expert_ids_keys = jax.random.split(jax.random.fold_in(part_keys[4], 1), TOKENS // REQ_DEV)
    expert_ids_turns = jax.random.permutation(jax.random.fold_in(part_keys[4], 3), TOKENS // REQ_DEV)
    expert_ids = jax.vmap(lambda own, number: deal_out(jax.random.fold_in(part_keys[4], 2), own, number, REQ_DEV, EXPERTS, TOPK, CAP, 2))(expert_ids_keys, expert_ids_turns).reshape((TOKENS, TOPK))
    route_weights = jnp.clip(jnp.exp(math.log(1.0) - 2.3025851 * jax.random.uniform(part_keys[5], (TOKENS, TOPK), jnp.float32) ** levels(part_keys[5], (TOKENS, TOPK), ((0, 16),), -0.2, 0.2)), 0.1, 1.0)
    w_gate = gaussian(streams_of[6], (EXPERTS * FF, D), D ** -0.5, 0.0625, ((0, 16),))
    w_up = gaussian(streams_of[7], (EXPERTS * FF, D), D ** -0.5, 0.0625, ((0, 16),))
    w_down = gaussian(streams_of[8], (EXPERTS * FF, D), FF ** -0.5, 0.125, ((0, 16),))
    return {"queries": queries, "kv_cache": kv_cache, "kv_lengths": kv_lengths, "moe_input": moe_input, "expert_ids": expert_ids, "route_weights": route_weights, "w_gate": w_gate, "w_up": w_up, "w_down": w_down}


score_scale = 192.0 ** -0.5


def reference(queries, kv_cache, kv_lengths, moe_input, expert_ids, route_weights, w_gate, w_up, w_down):
    query_wide = queries.astype(jnp.float32)
    cache_wide = kv_cache.astype(jnp.float32)
    scores = jnp.einsum("thk,tlk->thl", query_wide, cache_wide) * score_scale
    slot_index = jnp.arange(LMAX, dtype=jnp.int32)
    usable = slot_index[None, None, :] < kv_lengths[:, None, None]
    scores = jnp.where(usable, scores, -1e30)
    row_max = jnp.max(scores, axis=2, keepdims=True)
    raw_weights = jnp.where(usable, jnp.exp(scores - row_max), 0.0)
    probs = (raw_weights / jnp.sum(raw_weights, axis=2, keepdims=True)).astype(jnp.bfloat16)
    attended = jnp.einsum("thl,tlk->thk", probs.astype(jnp.float32), cache_wide[:, :, :LAT]).astype(jnp.bfloat16)

    rows_total = N_EP * CAP
    contract = (((1,), (1,)), ((), ()))

    def one_expert(expert):
        matches = expert_ids == expert
        chosen = jnp.any(matches, axis=1)
        weight = jnp.sum(jnp.where(matches, route_weights, 0.0), axis=1)
        ordering = jnp.argsort(jnp.where(chosen, 0, 1).astype(jnp.int32), stable=True)[:rows_total].astype(jnp.int32)
        picked = moe_input[ordering]
        first_row = (expert * FF).astype(jnp.int32)
        gate_rows = lax.dynamic_slice_in_dim(w_gate, first_row, FF, 0)
        up_rows = lax.dynamic_slice_in_dim(w_up, first_row, FF, 0)
        down_rows = lax.dynamic_slice_in_dim(w_down, first_row, FF, 0)
        gate_act = lax.dot_general(picked, gate_rows, contract, preferred_element_type=jnp.float32)
        up_act = lax.dot_general(picked, up_rows, contract, preferred_element_type=jnp.float32)
        hidden = (jax.nn.silu(gate_act) * up_act).astype(jnp.bfloat16)
        expert_out = jnp.dot(hidden, down_rows, preferred_element_type=jnp.float32)
        return ordering, expert_out * weight[ordering][:, None]

    orderings, outputs = lax.map(one_expert, jnp.arange(EXPERTS, dtype=jnp.int32))
    combined = jnp.zeros((moe_input.shape[0], D), jnp.float32)
    combined = combined.at[orderings.reshape(-1)].add(outputs.reshape(-1, D))
    return attended, combined.astype(jnp.bfloat16)
```

```python
import functools

import jax
import jax.numpy as jnp
from jax import lax
from jax.experimental import pallas as pl
from jax.experimental.pallas import tpu as pltpu
from jax.sharding import PartitionSpec as P

LAT = 512
EXPERTS = 16
LANES = 128
HIDDEN_TILE = 256
COLUMN_TILE = 1024
SLOTS = 4

score_scale = 192.0 ** (-0.5)
rows_by_rows = (((1,), (1,)), ((), ()))


def attend_latent(queries, kv_cache, kv_lengths):
    scores = (
        jnp.einsum("rhk,rlk->rhl", queries, kv_cache, preferred_element_type=jnp.float32)
        * score_scale
    )
    slot_index = lax.broadcasted_iota(jnp.int32, scores.shape, 2)
    usable = slot_index < kv_lengths[:, None, None]
    scores = jnp.where(usable, scores, -1e30)
    row_max = jnp.max(scores, axis=2, keepdims=True)
    raw_weights = jnp.where(usable, jnp.exp(scores - row_max), 0.0)
    probs = (raw_weights / jnp.sum(raw_weights, axis=2, keepdims=True)).astype(jnp.bfloat16)
    values = kv_cache[:, :, :LAT]
    return jnp.einsum("rhl,rlk->rhk", probs, values, preferred_element_type=jnp.float32).astype(
        jnp.bfloat16
    )


def largest_tile(size, unit, most):
    return max(t for t in range(unit, min(size, most) + 1, unit) if size % t == 0)


def expert_kernel(width, hidden, expert_ref, own_ref, other_ref, *refs):
    w_gate, w_up, w_down, keep_ref, send_ref = refs[:5]
    tokens, gate_act, hid, row_buf, col_buf, row_sem, col_sem = refs[5:]
    half = own_ref.shape[0]
    tile, columns = row_buf.shape[1], col_buf.shape[2]
    row_slots, col_slots = row_buf.shape[0], col_buf.shape[0]
    row_tiles = 2 * (hidden // tile)
    col_tiles = width // columns

    def fetch(item):
        if item < row_tiles:
            source = (w_gate, w_up)[item % 2].at[pl.ds((item // 2) * tile, tile), :]
            slot = item % row_slots
            return pltpu.make_async_copy(source, row_buf.at[slot], row_sem.at[slot])
        item -= row_tiles
        slot = item % col_slots
        source = w_down.at[:, pl.ds(item * columns, columns)]
        return pltpu.make_async_copy(source, col_buf.at[slot], col_sem.at[slot])

    ahead = min(row_slots, col_slots)
    items = row_tiles + col_tiles
    for item in range(min(ahead, items)):
        fetch(item).start()
    tokens[pl.ds(0, half), :] = own_ref[...]
    tokens[pl.ds(half, half), :] = other_ref[...]

    for item in range(row_tiles):
        fetch(item).wait()
        act = lax.dot_general(
            tokens[:, pl.ds(0, width)],
            row_buf[item % row_slots],
            rows_by_rows,
            preferred_element_type=jnp.float32,
        )
        if item + ahead < items:
            fetch(item + ahead).start()
        if item % 2 == 0:
            gate_act[...] = act
        else:
            gated = gate_act[...]
            hid[:, pl.ds((item // 2) * tile, tile)] = (
                gated / (1.0 + jnp.exp(-gated)) * act
            ).astype(hid.dtype)

    extra = tokens[:, pl.ds(width, LANES)].astype(jnp.float32)
    lane = lax.broadcasted_iota(jnp.int32, extra.shape, 1)
    expert = expert_ref[0]
    mine = (lane == expert) | (lane == expert + EXPERTS)
    scale = jnp.sum(jnp.where(mine, extra, 0.0), axis=1, keepdims=True)

    for tile_id in range(col_tiles):
        item = row_tiles + tile_id
        fetch(item).wait()
        partial = jnp.dot(
            hid[...], col_buf[tile_id % col_slots], preferred_element_type=jnp.float32
        )
        if item + ahead < items:
            fetch(item + ahead).start()
        partial = partial * scale
        where = pl.ds(tile_id * columns, columns)
        keep_ref[:, where] = partial[:half]
        send_ref[:, where] = partial[half:].astype(send_ref.dtype)


def run_expert(expert, own, other, w_gate, w_up, w_down):
    half = own.shape[0]
    hidden, width = w_down.shape
    tile = largest_tile(hidden, LANES, HIDDEN_TILE)
    columns = largest_tile(width, LANES, COLUMN_TILE)
    in_vmem = pl.BlockSpec(memory_space=pltpu.VMEM)
    in_place = pl.BlockSpec(memory_space=pl.ANY)
    return pl.pallas_call(
        functools.partial(expert_kernel, width, hidden),
        out_shape=(
            jax.ShapeDtypeStruct((half, width), jnp.float32),
            jax.ShapeDtypeStruct((half, width), own.dtype),
        ),
        in_specs=[pl.BlockSpec(memory_space=pltpu.SMEM), in_vmem, in_vmem] + [in_place] * 3,
        out_specs=(in_vmem, in_vmem),
        scratch_shapes=[
            pltpu.VMEM((2 * half, own.shape[1]), own.dtype),
            pltpu.VMEM((2 * half, tile), jnp.float32),
            pltpu.VMEM((2 * half, hidden), own.dtype),
            pltpu.VMEM((SLOTS, tile, width), w_gate.dtype),
            pltpu.VMEM((SLOTS, hidden, columns), w_down.dtype),
            pltpu.SemaphoreType.DMA((SLOTS,)),
            pltpu.SemaphoreType.DMA((SLOTS,)),
        ],
        compiler_params=pltpu.CompilerParams(vmem_limit_bytes=44 << 20),
        cost_estimate=pl.CostEstimate(
            flops=12 * half * hidden * width,
            bytes_accessed=6 * hidden * width,
            transcendentals=2 * half * hidden,
        ),
        name="expert",
    )(expert, own, other, w_gate, w_up, w_down)


def swap(value, mask, devices):
    return lax.ppermute(value, "ep", [(i, i ^ mask) for i in range(devices)])


def local(
    queries, kv_cache, kv_lengths, moe_input, expert_ids, route_weights, w_gate, w_up, w_down
):
    attended = attend_latent(queries, kv_cache, kv_lengths)
    devices = lax.axis_size("ep")
    slices = devices // EXPERTS
    requests = moe_input.shape[0]

    experts_iota = jnp.arange(EXPERTS, dtype=jnp.int32)
    matches = expert_ids[:, :, None] == experts_iota[None, None, :]
    dense = jnp.sum(jnp.where(matches, route_weights[:, :, None], 0.0), axis=1)
    high = lax.reduce_precision(dense, 8, 7)
    parts = jnp.concatenate(
        [high, dense - high, jnp.zeros((requests, LANES - 2 * EXPERTS), jnp.float32)], axis=1
    )
    rows = jnp.concatenate([moe_input, parts.astype(moe_input.dtype)], axis=1)

    masks = [1 << bit for bit in range(devices.bit_length() - 1)]
    for mask in reversed(masks[1:]):
        rows = jnp.concatenate([rows, swap(rows, mask, devices)], axis=0)
    other = swap(rows, masks[0], devices)

    expert = (lax.axis_index("ep") // slices).astype(jnp.int32).reshape(1)
    keep, send = run_expert(expert, rows, other, w_gate, w_up, w_down)
    total = keep + swap(send, masks[0], devices).astype(jnp.float32)
    for mask in masks[1:]:
        half = total.shape[0] // 2
        arrived = swap(total[half:].astype(moe_input.dtype), mask, devices)
        total = total[:half] + arrived.astype(jnp.float32)
    return (attended, total.astype(jnp.bfloat16))


def solution(mesh):
    in_specs = (
        P(("groups", "ep"), None, None),
        P(("groups", "ep"), None, None),
        P(("groups", "ep")),
        P(("groups", "ep"), None),
        P(("groups", "ep"), None),
        P(("groups", "ep"), None),
        P("ep", None),
        P("ep", None),
        P("ep", None),
    )
    out_specs = (P(("groups", "ep"), None, None), P(("groups", "ep"), None))
    return jax.shard_map(local, mesh=mesh, in_specs=in_specs, out_specs=out_specs, check_vma=False)
```

```python
import jax
import jax.numpy as jnp
from jax import lax
from jax.experimental import pallas as pl
from jax.experimental.pallas import tpu as pltpu
from jax.sharding import PartitionSpec as P


LAT = 512
EXPERTS = 16
LANES = 128
HIDDEN_TILE = 512
COLUMN_TILE = 1024
SLOTS = 4
EXPERT_VMEM = 38 << 20

score_scale = 192.0 ** (-0.5)
rows_by_rows = (((1,), (1,)), ((), ()))


def attend_latent(queries, kv_cache, kv_lengths):
    scores = (
        jnp.einsum("rhk,rlk->rhl", queries, kv_cache, preferred_element_type=jnp.float32)
        * score_scale
    )
    slot_index = lax.broadcasted_iota(jnp.int32, scores.shape, 2)
    usable = slot_index < kv_lengths[:, None, None]
    scores = jnp.where(usable, scores, -1e30)
    row_max = jnp.max(scores, axis=2, keepdims=True)
    raw_weights = jnp.where(usable, jnp.exp(scores - row_max), 0.0)
    probs = (raw_weights / jnp.sum(raw_weights, axis=2, keepdims=True)).astype(jnp.bfloat16)
    values = kv_cache[:, :, :LAT]
    return jnp.einsum("rhl,rlk->rhk", probs, values, preferred_element_type=jnp.float32).astype(
        jnp.bfloat16
    )


def largest_tile(size, unit, most):
    return max(t for t in range(unit, min(size, most) + 1, unit) if size % t == 0)


def pack_kernel(inputs, ids, weights, out_ref, inputs_ref, ids_ref, weights_ref, sem):
    requests, width = inputs_ref.shape
    pairs = ((ids, ids_ref), (weights, weights_ref), (inputs, inputs_ref))
    copies = [
        pltpu.make_async_copy(source, target, sem.at[i])
        for i, (source, target) in enumerate(pairs)
    ]
    for copy in copies:
        copy.start()
    for copy in copies:
        copy.wait()
    out_ref[:, pl.ds(0, width)] = inputs_ref[...]
    lane = lax.broadcasted_iota(jnp.int32, (requests, LANES), 1)
    expert = jnp.where(lane < EXPERTS, lane, lane - EXPERTS)
    dense = jnp.zeros((requests, LANES), jnp.float32)
    for route in range(ids_ref.shape[1]):
        named = expert == ids_ref[:, route : route + 1]
        dense = dense + jnp.where(named, weights_ref[:, route : route + 1], 0.0)
    high = dense.astype(out_ref.dtype).astype(jnp.float32)
    low = jnp.where(lane < 2 * EXPERTS, dense - high, 0.0)
    parts = jnp.where(lane < EXPERTS, high, low)
    out_ref[:, pl.ds(width, LANES)] = parts.astype(out_ref.dtype)


def pack(moe_input, expert_ids, route_weights):
    requests, width = moe_input.shape
    operands = (moe_input, expert_ids, route_weights)
    return pl.pallas_call(
        pack_kernel,
        out_shape=jax.ShapeDtypeStruct((requests, width + LANES), moe_input.dtype),
        in_specs=[pl.BlockSpec(memory_space=pltpu.HBM)] * 3,
        out_specs=pl.BlockSpec(memory_space=pltpu.VMEM),
        scratch_shapes=[pltpu.VMEM(operand.shape, operand.dtype) for operand in operands]
        + [pltpu.SemaphoreType.DMA((3,))],
        compiler_params=pltpu.CompilerParams(vmem_limit_bytes=8 << 20),
        cost_estimate=pl.CostEstimate(
            flops=0, bytes_accessed=4 * requests * width, transcendentals=0
        ),
        name="pack",
    )(*(pltpu.with_memory_space_constraint(operand, pltpu.HBM) for operand in operands))


def preload_kernel(expert_ref, source, target, sem):
    copy = pltpu.make_async_copy(source.at[pl.ds(0, target.shape[0]), :], target, sem)
    copy.start()
    copy.wait()


def preload(expert, source, tile):
    width = source.shape[1]
    return pl.pallas_call(
        preload_kernel,
        out_shape=jax.ShapeDtypeStruct((tile, width), source.dtype),
        in_specs=[pl.BlockSpec(memory_space=pltpu.SMEM), pl.BlockSpec(memory_space=pltpu.HBM)],
        out_specs=pl.BlockSpec(memory_space=pltpu.VMEM),
        scratch_shapes=[pltpu.SemaphoreType.DMA],
        compiler_params=pltpu.CompilerParams(vmem_limit_bytes=40 << 20),
        cost_estimate=pl.CostEstimate(
            flops=0, bytes_accessed=2 * tile * width, transcendentals=0
        ),
        name="preload",
    )(expert, source)


def join_kernel(own_ref, other_ref, out_ref):
    half = own_ref.shape[0]
    out_ref[pl.ds(0, half), :] = own_ref[...]
    out_ref[pl.ds(half, half), :] = other_ref[...]


def join(own, other):
    half, width = own.shape
    in_vmem = pl.BlockSpec(memory_space=pltpu.VMEM)
    return pl.pallas_call(
        join_kernel,
        out_shape=jax.ShapeDtypeStruct((2 * half, width), own.dtype),
        in_specs=[in_vmem, in_vmem],
        out_specs=in_vmem,
        compiler_params=pltpu.CompilerParams(vmem_limit_bytes=16 << 20),
        cost_estimate=pl.CostEstimate(
            flops=0, bytes_accessed=8 * half * width, transcendentals=0
        ),
        name="join",
    )(own, other)


def expert_kernel(expert_ref, own_ref, other_ref, *refs):
    first_gate, first_up, w_gate, w_up, w_down, keep_ref, send_ref = refs[:7]
    tokens, gate_act, hid, total, buf, sem = refs[7:]
    half, width = keep_ref.shape
    slots, tile, _ = buf.shape
    sources = (w_gate, w_up, w_down)
    loaded = (first_gate, first_up)
    tiles = w_down.shape[0] // tile
    items = len(sources) * tiles
    columns = largest_tile(width, LANES, COLUMN_TILE)

    def fetch(item):
        kind, slot = item % len(sources), item % slots
        source = sources[kind].at[pl.ds((item // len(sources)) * tile, tile), :]
        return pltpu.make_async_copy(source, buf.at[slot], sem.at[slot])

    for item in range(len(loaded), min(len(loaded) + slots, items)):
        fetch(item).start()
    tokens[pl.ds(0, half), :] = own_ref[...]
    tokens[pl.ds(half, half), :] = other_ref[...]

    extra = tokens[:, pl.ds(width, LANES)].astype(jnp.float32)
    lane = lax.broadcasted_iota(jnp.int32, extra.shape, 1)
    expert = expert_ref[0]
    mine = (lane == expert) | (lane == expert + EXPERTS)
    scale = jnp.sum(jnp.where(mine, extra, 0.0), axis=1, keepdims=True)

    for item in range(items):
        if item >= len(loaded):
            fetch(item).wait()
        weights = loaded[item] if item < len(loaded) else buf.at[item % slots]
        kind, index = item % len(sources), item // len(sources)
        if kind < 2:
            act = lax.dot_general(
                tokens[:, pl.ds(0, width)],
                weights[...],
                rows_by_rows,
                preferred_element_type=jnp.float32,
            )
            if kind == 0:
                gate_act[...] = act
            else:
                gated = gate_act[...]
                hid[...] = (gated / (1.0 + jnp.exp(-gated)) * act).astype(hid.dtype)
        else:
            for start in range(0, width, columns):
                where = pl.ds(start, columns)
                partial = jnp.dot(
                    hid[...], weights[:, where], preferred_element_type=jnp.float32
                )
                if index > 0:
                    partial = partial + total[:, where]
                if index < tiles - 1:
                    total[:, where] = partial
                else:
                    partial = partial * scale
                    keep_ref[:, where] = partial[:half]
                    send_ref[:, where] = partial[half:].astype(send_ref.dtype)
        if item >= len(loaded) and item + slots < items:
            fetch(item + slots).start()


def run_expert(expert, own, other, loaded, w_gate, w_up, w_down):
    half = own.shape[0]
    hidden, width = w_down.shape
    tile = loaded[0].shape[0]
    in_vmem = pl.BlockSpec(memory_space=pltpu.VMEM)
    in_place = pl.BlockSpec(memory_space=pltpu.HBM)
    return pl.pallas_call(
        expert_kernel,
        out_shape=(
            jax.ShapeDtypeStruct((half, width), jnp.float32),
            jax.ShapeDtypeStruct((half, width), own.dtype),
        ),
        in_specs=[pl.BlockSpec(memory_space=pltpu.SMEM)] + [in_vmem] * 4 + [in_place] * 3,
        out_specs=(in_vmem, in_vmem),
        scratch_shapes=[
            pltpu.VMEM((2 * half, own.shape[1]), own.dtype),
            pltpu.VMEM((2 * half, tile), jnp.float32),
            pltpu.VMEM((2 * half, tile), own.dtype),
            pltpu.VMEM((2 * half, width), jnp.float32),
            pltpu.VMEM((SLOTS, tile, width), w_gate.dtype),
            pltpu.SemaphoreType.DMA((SLOTS,)),
        ],
        compiler_params=pltpu.CompilerParams(vmem_limit_bytes=EXPERT_VMEM),
        cost_estimate=pl.CostEstimate(
            flops=12 * half * hidden * width,
            bytes_accessed=6 * hidden * width,
            transcendentals=2 * half * hidden,
        ),
        name="expert",
    )(expert, own, other, *loaded, w_gate, w_up, w_down)


def swap(value, mask, devices):
    return lax.ppermute(value, "ep", [(i, i ^ mask) for i in range(devices)])


def layer(
    queries, kv_cache, kv_lengths, moe_input, expert_ids, route_weights, w_gate, w_up, w_down
):
    attended = attend_latent(queries, kv_cache, kv_lengths)
    devices = lax.axis_size("ep")
    slices = devices // EXPERTS

    rows = pack(moe_input, expert_ids, route_weights)
    expert = (lax.axis_index("ep") // slices).astype(jnp.int32).reshape(1)
    tile = largest_tile(w_gate.shape[0], LANES, HIDDEN_TILE)
    first_gate = preload(expert, w_gate, tile)
    first_up = preload(expert, w_up, tile)
    loaded = (first_gate, first_up)

    masks = [1 << bit for bit in range(devices.bit_length() - 1)]
    for mask in reversed(masks[1:]):
        arrived = swap(rows, mask, devices)
        if mask in masks[1:3]:
            rows = join(rows, arrived)
        else:
            rows = jnp.concatenate([rows, arrived], axis=0)
    other = swap(rows, masks[0], devices)

    keep, send = run_expert(expert, rows, other, loaded, w_gate, w_up, w_down)
    total = keep + swap(send, masks[0], devices).astype(jnp.float32)
    for mask in masks[1:]:
        half = total.shape[0] // 2
        arrived = swap(total[half:].astype(moe_input.dtype), mask, devices)
        total = total[:half] + arrived.astype(jnp.float32)
    return (attended, total.astype(jnp.bfloat16))


def solution(mesh):
    in_specs = (
        P(("groups", "ep"), None, None),
        P(("groups", "ep"), None, None),
        P(("groups", "ep")),
        P(("groups", "ep"), None),
        P(("groups", "ep"), None),
        P(("groups", "ep"), None),
        P("ep", None),
        P("ep", None),
        P("ep", None),
    )
    out_specs = (P(("groups", "ep"), None, None), P(("groups", "ep"), None))
    return jax.shard_map(layer, mesh=mesh, in_specs=in_specs, out_specs=out_specs, check_vma=False)
```

```python
import functools

import jax
import jax.numpy as jnp
from jax import lax
from jax.experimental import pallas as pl
from jax.experimental.pallas import tpu as pltpu
from jax.sharding import PartitionSpec as P


LAT = 512
EXPERTS = 16
LANES = 128
HIDDEN_TILE = 512
COLUMN_TILE = 1024
SLOTS = 4
EXPERT_VMEM = 38 << 20

score_scale = 192.0 ** (-0.5)
rows_by_rows = (((1,), (1,)), ((), ()))


def attend_latent(queries, kv_cache, kv_lengths):
    scores = (
        jnp.einsum("rhk,rlk->rhl", queries, kv_cache, preferred_element_type=jnp.float32)
        * score_scale
    )
    slot_index = lax.broadcasted_iota(jnp.int32, scores.shape, 2)
    usable = slot_index < kv_lengths[:, None, None]
    scores = jnp.where(usable, scores, -1e30)
    row_max = jnp.max(scores, axis=2, keepdims=True)
    raw_weights = jnp.where(usable, jnp.exp(scores - row_max), 0.0)
    probs = (raw_weights / jnp.sum(raw_weights, axis=2, keepdims=True)).astype(jnp.bfloat16)
    values = kv_cache[:, :, :LAT]
    return jnp.einsum("rhl,rlk->rhk", probs, values, preferred_element_type=jnp.float32).astype(
        jnp.bfloat16
    )


def largest_tile(size, unit, most):
    return max(t for t in range(unit, min(size, most) + 1, unit) if size % t == 0)


def pack_kernel(inputs, ids, weights, out_ref, inputs_ref, ids_ref, weights_ref, sem):
    requests, width = inputs_ref.shape
    pairs = ((ids, ids_ref), (weights, weights_ref), (inputs, inputs_ref))
    copies = [
        pltpu.make_async_copy(source, target, sem.at[i])
        for i, (source, target) in enumerate(pairs)
    ]
    for copy in copies:
        copy.start()
    for copy in copies:
        copy.wait()
    out_ref[:, pl.ds(0, width)] = inputs_ref[...]
    lane = lax.broadcasted_iota(jnp.int32, (requests, LANES), 1)
    expert = jnp.where(lane < EXPERTS, lane, lane - EXPERTS)
    dense = jnp.zeros((requests, LANES), jnp.float32)
    for route in range(ids_ref.shape[1]):
        named = expert == ids_ref[:, route : route + 1]
        dense = dense + jnp.where(named, weights_ref[:, route : route + 1], 0.0)
    high = dense.astype(out_ref.dtype).astype(jnp.float32)
    low = jnp.where(lane < 2 * EXPERTS, dense - high, 0.0)
    parts = jnp.where(lane < EXPERTS, high, low)
    out_ref[:, pl.ds(width, LANES)] = parts.astype(out_ref.dtype)


def pack(moe_input, expert_ids, route_weights):
    requests, width = moe_input.shape
    operands = (moe_input, expert_ids, route_weights)
    return pl.pallas_call(
        pack_kernel,
        out_shape=jax.ShapeDtypeStruct((requests, width + LANES), moe_input.dtype),
        in_specs=[pl.BlockSpec(memory_space=pltpu.HBM)] * 3,
        out_specs=pl.BlockSpec(memory_space=pltpu.VMEM),
        scratch_shapes=[pltpu.VMEM(operand.shape, operand.dtype) for operand in operands]
        + [pltpu.SemaphoreType.DMA((3,))],
        compiler_params=pltpu.CompilerParams(vmem_limit_bytes=8 << 20),
        cost_estimate=pl.CostEstimate(
            flops=0, bytes_accessed=4 * requests * width, transcendentals=0
        ),
        name="pack",
    )(*(pltpu.with_memory_space_constraint(operand, pltpu.HBM) for operand in operands))


def preload_kernel(start, expert_ref, source, target, sem):
    copy = pltpu.make_async_copy(source.at[pl.ds(start, target.shape[0]), :], target, sem)
    copy.start()
    copy.wait()


def preload(expert, source, start, tile):
    width = source.shape[1]
    return pl.pallas_call(
        functools.partial(preload_kernel, start),
        out_shape=jax.ShapeDtypeStruct((tile, width), source.dtype),
        in_specs=[pl.BlockSpec(memory_space=pltpu.SMEM), pl.BlockSpec(memory_space=pltpu.HBM)],
        out_specs=pl.BlockSpec(memory_space=pltpu.VMEM),
        scratch_shapes=[pltpu.SemaphoreType.DMA],
        compiler_params=pltpu.CompilerParams(vmem_limit_bytes=40 << 20),
        cost_estimate=pl.CostEstimate(
            flops=0, bytes_accessed=2 * tile * width, transcendentals=0
        ),
        name="preload",
    )(expert, source)


def join_kernel(own_ref, other_ref, out_ref):
    half = own_ref.shape[0]
    out_ref[pl.ds(0, half), :] = own_ref[...]
    out_ref[pl.ds(half, half), :] = other_ref[...]


def join(own, other):
    half, width = own.shape
    in_vmem = pl.BlockSpec(memory_space=pltpu.VMEM)
    return pl.pallas_call(
        join_kernel,
        out_shape=jax.ShapeDtypeStruct((2 * half, width), own.dtype),
        in_specs=[in_vmem, in_vmem],
        out_specs=in_vmem,
        compiler_params=pltpu.CompilerParams(vmem_limit_bytes=16 << 20),
        cost_estimate=pl.CostEstimate(
            flops=0, bytes_accessed=8 * half * width, transcendentals=0
        ),
        name="join",
    )(own, other)


def expert_kernel(expert_ref, own_ref, other_ref, *refs):
    lower_gate, upper_gate, first_up, w_gate, w_up, w_down, keep_ref, send_ref = refs[:8]
    tokens, gate_act, hid, total, buf, sem = refs[8:]
    half, width = keep_ref.shape
    slots, tile, _ = buf.shape
    sources = (w_gate, w_up, w_down)
    loaded = ((lower_gate, upper_gate), (first_up,))
    tiles = w_down.shape[0] // tile
    items = len(sources) * tiles
    columns = largest_tile(width, LANES, COLUMN_TILE)

    def fetch(item):
        kind, slot = item % len(sources), item % slots
        source = sources[kind].at[pl.ds((item // len(sources)) * tile, tile), :]
        return pltpu.make_async_copy(source, buf.at[slot], sem.at[slot])

    for item in range(len(loaded), min(len(loaded) + slots, items)):
        fetch(item).start()
    tokens[pl.ds(0, half), :] = own_ref[...]
    tokens[pl.ds(half, half), :] = other_ref[...]

    extra = tokens[:, pl.ds(width, LANES)].astype(jnp.float32)
    lane = lax.broadcasted_iota(jnp.int32, extra.shape, 1)
    expert = expert_ref[0]
    mine = (lane == expert) | (lane == expert + EXPERTS)
    scale = jnp.sum(jnp.where(mine, extra, 0.0), axis=1, keepdims=True)

    for item in range(items):
        if item >= len(loaded):
            fetch(item).wait()
        pieces = loaded[item] if item < len(loaded) else (buf.at[item % slots],)
        weights = pieces[0]
        kind, index = item % len(sources), item // len(sources)
        if kind < 2:
            acts = [
                lax.dot_general(
                    tokens[:, pl.ds(0, width)],
                    piece[...],
                    rows_by_rows,
                    preferred_element_type=jnp.float32,
                )
                for piece in pieces
            ]
            act = jnp.concatenate(acts, axis=1) if len(acts) > 1 else acts[0]
            if kind == 0:
                gate_act[...] = act
            else:
                gated = gate_act[...]
                hid[...] = (gated / (1.0 + jnp.exp(-gated)) * act).astype(hid.dtype)
        else:
            for start in range(0, width, columns):
                where = pl.ds(start, columns)
                partial = jnp.dot(
                    hid[...], weights[:, where], preferred_element_type=jnp.float32
                )
                if index > 0:
                    partial = partial + total[:, where]
                if index < tiles - 1:
                    total[:, where] = partial
                else:
                    partial = partial * scale
                    keep_ref[:, where] = partial[:half]
                    send_ref[:, where] = partial[half:].astype(send_ref.dtype)
        if item >= len(loaded) and item + slots < items:
            fetch(item + slots).start()


def run_expert(expert, own, other, loaded, w_gate, w_up, w_down):
    half = own.shape[0]
    hidden, width = w_down.shape
    tile = loaded[-1].shape[0]
    in_vmem = pl.BlockSpec(memory_space=pltpu.VMEM)
    in_place = pl.BlockSpec(memory_space=pltpu.HBM)
    return pl.pallas_call(
        expert_kernel,
        out_shape=(
            jax.ShapeDtypeStruct((half, width), jnp.float32),
            jax.ShapeDtypeStruct((half, width), own.dtype),
        ),
        in_specs=[pl.BlockSpec(memory_space=pltpu.SMEM)] + [in_vmem] * 5 + [in_place] * 3,
        out_specs=(in_vmem, in_vmem),
        scratch_shapes=[
            pltpu.VMEM((2 * half, own.shape[1]), own.dtype),
            pltpu.VMEM((2 * half, tile), jnp.float32),
            pltpu.VMEM((2 * half, tile), own.dtype),
            pltpu.VMEM((2 * half, width), jnp.float32),
            pltpu.VMEM((SLOTS, tile, width), w_gate.dtype),
            pltpu.SemaphoreType.DMA((SLOTS,)),
        ],
        compiler_params=pltpu.CompilerParams(vmem_limit_bytes=EXPERT_VMEM),
        cost_estimate=pl.CostEstimate(
            flops=12 * half * hidden * width,
            bytes_accessed=6 * hidden * width,
            transcendentals=2 * half * hidden,
        ),
        name="expert",
    )(expert, own, other, *loaded, w_gate, w_up, w_down)


def swap(value, mask, devices):
    return lax.ppermute(value, "ep", [(i, i ^ mask) for i in range(devices)])


def layer(
    queries, kv_cache, kv_lengths, moe_input, expert_ids, route_weights, w_gate, w_up, w_down
):
    attended = attend_latent(queries, kv_cache, kv_lengths)
    devices = lax.axis_size("ep")
    slices = devices // EXPERTS

    rows = pack(moe_input, expert_ids, route_weights)
    expert = (lax.axis_index("ep") // slices).astype(jnp.int32).reshape(1)
    tile = largest_tile(w_gate.shape[0], LANES, HIDDEN_TILE)
    lower_gate = preload(expert, w_gate, 0, tile // 2)
    upper_gate = preload(expert, w_gate, tile // 2, tile // 2)
    first_up = preload(expert, w_up, 0, tile)
    loaded = (lower_gate, upper_gate, first_up)

    masks = [1 << bit for bit in range(devices.bit_length() - 1)]
    for mask in reversed(masks[1:]):
        arrived = swap(rows, mask, devices)
        if mask in masks[1:4]:
            rows = join(rows, arrived)
        else:
            rows = jnp.concatenate([rows, arrived], axis=0)
    other = swap(rows, masks[0], devices)

    keep, send = run_expert(expert, rows, other, loaded, w_gate, w_up, w_down)
    total = keep + swap(send, masks[0], devices).astype(jnp.float32)
    for mask in masks[1:]:
        half = total.shape[0] // 2
        arrived = swap(total[half:].astype(moe_input.dtype), mask, devices)
        total = total[:half] + arrived.astype(jnp.float32)
    return (attended, total.astype(jnp.bfloat16))


def solution(mesh):
    in_specs = (
        P(("groups", "ep"), None, None),
        P(("groups", "ep"), None, None),
        P(("groups", "ep")),
        P(("groups", "ep"), None),
        P(("groups", "ep"), None),
        P(("groups", "ep"), None),
        P("ep", None),
        P("ep", None),
        P("ep", None),
    )
    out_specs = (P(("groups", "ep"), None, None), P(("groups", "ep"), None))
    return jax.shard_map(layer, mesh=mesh, in_specs=in_specs, out_specs=out_specs, check_vma=False)
```
